128 devices in a mesh: row: 16 (over x, y_hi, core), col: 8 (over z, y_lo).
Axes of the slice: x: 4, y: 4 (y_hi: 2, y_lo: 2; y = y_hi * 2 + y_lo), z: 4, core: 2. Of those that a mesh axis runs over, the one named last changes fastest.
Arguments:
- object_field: float32 [2, 8192, 4096], P(None, 'row', 'col'), may hold values from -6 to 6
- probe: float32 [3, 2, 256, 256], replicated, may hold values from -6 to 6
- raw_counts: bfloat16 [768, 256, 256], P(('row', 'col')), may hold values from 0.099609375 to 10
- resample_delta: float32 [256, 256], replicated, may hold values from -0.1875 to 0.1875
- tile_row: int32 [768, 1], P(('row', 'col')), may hold values from 0 to 15; in each aligned block of 6 rows (0 to 5, 6 to 11, ...) no two rows name the same one
- offsets: int32 [768, 2], P(('row', 'col')), may hold values from 0 to 511
Outputs:
- object_grad: float32 [2, 8192, 4096], P(None, 'row', 'col')
- probe_grad: float32 [3, 2, 256, 256], replicated
The draws below stay inside these ranges and needn't reach their ends.
Inputs may be any that keep to these rules, and one draw needn't show every extreme that they name: `tile_row`: the 6 frames of one device have distinct tile rows.
All inputs are finite; a program needn't handle non-finite values.
Results may differ from the reference program's by a relative error of at most 0.0008.
The reference program's roundings to bfloat16 on the way count: a program that leaves them out, or rounds other values in their place, can miss the bound.
Values may be sent and summed in bfloat16 or wider, within the bound.
No kernel may reach another device: no remote copies, remote signals or barrier semaphores. Data moves between devices by JAX's collectives and lax.ppermute only.
A program may use at most 128 MiB of HBM per device.

```python
import math
import jax
import jax.numpy as jnp
import numpy as np
from jax import lax

FRAME = 256
MODES = 3
TILE = 512
FR_DEV = 6
FRAMES = 768
OBJ_ROWS = 8192
OBJ_COLS = 4096
N_ROW = 16
N_COL = 8


def set_ends(entries, rng, low, high):
    place = [jax.random.randint(jax.random.fold_in(rng, axis), (), 0, length) for axis, length in enumerate(entries.shape)]
    longest = entries.shape.index(max(entries.shape))
    next_to = place[:longest] + [(place[longest] + 1) % entries.shape[longest]] + place[longest + 1:]
    return entries.at[tuple(place)].set(low).at[tuple(next_to)].set(high)


def level_of(stream_key, shape, pieces, least, largest):
    def one(axis_at, parts):
        steps = jax.random.uniform(jax.random.fold_in(jax.random.fold_in(stream_key, 6), axis_at), (parts,), jnp.float32, least / len(pieces), largest / len(pieces))
        return jnp.repeat(jnp.exp(steps), shape[axis_at] // parts).reshape((-1,) + (1,) * (len(shape) - axis_at - 1))

    loudness = one(*pieces[0])
    for cut in pieces[1:]:
        loudness = loudness * one(*cut)
    return loudness


def shared_out(key, own, number, rows, count, top, reach, skew):
    sequence = jax.random.permutation(key, count)
    packed, ordinary = shares(count, rows * top, reach, skew, True), shares(count, rows * top, reach, skew, False)
    places = jnp.arange(count)

    def named(lengths, turn):
        used = int((lengths > 0).sum())
        fixed = max(1, used // 4)
        shifted = fixed + (places - fixed + turn * (used - fixed)) % max(1, count - fixed)
        return jnp.zeros((count,), jnp.int32).at[sequence[jnp.where(places < fixed, places, shifted)]].set(jnp.asarray(lengths, jnp.int32))

    lengths = jnp.where(number % 4 == 0, named(packed, number // 4), named(ordinary, number - number // 4 - 1))
    mixed = jax.random.permutation(jax.random.fold_in(own, 3), count)
    giver, sink = mixed[0:count // 2 * 2:2], mixed[1:count // 2 * 2:2]
    margin = jnp.minimum(lengths[giver] - 1, reach - lengths[sink]) // 2
    margin = jnp.where((giver == sequence[0]) | (sink == sequence[0]) | (lengths[sink] == 0), 0, jnp.maximum(margin, 0))
    shifted = jax.random.randint(jax.random.fold_in(own, 4), (count // 2,), 0, 1 << 20) % (margin + 1)
    lengths = lengths.at[giver].add(-shifted).at[sink].add(shifted)
    items = jnp.searchsorted(jnp.cumsum(lengths), jnp.arange(rows * top), side="right").astype(jnp.int32)
    listing = items.reshape(top, rows).T
    listing = listing[jax.random.permutation(jax.random.fold_in(own, 1), rows)]
    turn = jax.random.randint(jax.random.fold_in(own, 2), (rows, 1), 0, top)
    return jnp.take_along_axis(listing, (jnp.arange(top)[None, :] + turn) % top, axis=1)


def shares(number_of, total, most, skew, full):
    loads = [(1 << 20) // math.isqrt(standing ** skew) + 1 for standing in range(1, number_of + 1)]
    largest = most if full else min(most, max(-(-total // number_of), total * loads[0] // sum(loads)))
    least = 1 if total - largest >= number_of - 1 else 0
    counts, surplus = [largest] + [least] * (number_of - 1), total - largest - least * (number_of - 1)
    while surplus > 0:
        movable = [i for i in range(1, number_of) if counts[i] < largest] or [i for i in range(1, number_of) if counts[i] < most]
        pool, budget = sum([loads[i] for i in movable]), surplus
        for i in movable:
            more = min(most - counts[i], max(1, budget * loads[i] // pool), surplus)
            counts[i] = counts[i] + more
            surplus = surplus - more
    return np.array(counts)


def bell_draw(stream_key, extent, width, bound, cuts=(), held_as=jnp.bfloat16):
    values = width * jax.random.normal(stream_key, extent, jnp.float32)
    if cuts:
        values = values * level_of(stream_key, extent, cuts, -0.22, 0.18)
    return jnp.clip(values, -bound, bound).astype(held_as)


def setup_inputs(seed: int = 0) -> dict:
    arg_keys = jax.random.split(jax.random.key(seed), 7)
    object_field = bell_draw(arg_keys[0], (2, OBJ_ROWS, OBJ_COLS), 1.0, 6.0, ((1, 16), (2, 8)), jnp.float32)
    probe = bell_draw(arg_keys[1], (MODES, 2, FRAME, FRAME), 1.0, 6.0, (), jnp.float32)
    raw_counts = jnp.clip(jnp.exp(math.log(10.0) - 4.609084 * jax.random.uniform(arg_keys[2], (FRAMES, FRAME, FRAME), jnp.float32) ** level_of(arg_keys[2], (FRAMES, FRAME, FRAME), ((0, 128),), -0.2, 0.2)), 0.099609375, 10.0).astype(jnp.bfloat16)
    resample_delta = bell_draw(arg_keys[3], (FRAME, FRAME), (4 * FRAME) ** -0.5, 0.1875, (), jnp.float32)
    tile_row_keys = jax.random.split(jax.random.fold_in(arg_keys[4], 1), FRAMES // FR_DEV)
    tile_row_turns = jax.random.permutation(jax.random.fold_in(arg_keys[4], 3), FRAMES // FR_DEV)
    tile_row = jax.vmap(lambda own, number: shared_out(jax.random.fold_in(arg_keys[4], 2), own, number, FR_DEV, N_ROW, 1, 1, 2))(tile_row_keys, tile_row_turns).reshape((FRAMES, 1))
    offsets = set_ends(jax.random.randint(arg_keys[5], (FRAMES, 2), 0, TILE), jax.random.fold_in(arg_keys[5], 1), 0, TILE - 1).astype(jnp.int32)
    return {"object_field": object_field, "probe": probe, "raw_counts": raw_counts, "resample_delta": resample_delta, "tile_row": tile_row, "offsets": offsets}


def product(left, right):
    return jnp.dot(left.astype(jnp.float32), right.astype(jnp.float32), preferred_element_type=jnp.float32)

def dft_tables(points):
    indices = jnp.arange(points, dtype=jnp.int32)
    phases = indices[:, None] * indices[None, :] % points
    angles = phases.astype(jnp.float32) * (2.0 * math.pi / points)
    norming = 1.0 / math.sqrt(points)
    cosine = jnp.cos(angles) * norming
    sine_part = -jnp.sin(angles) * norming
    forward = jnp.concatenate([jnp.concatenate([cosine, -sine_part], 1), jnp.concatenate([sine_part, cosine], 1)], 0)
    backward = jnp.concatenate([jnp.concatenate([cosine, sine_part], 1), jnp.concatenate([-sine_part, cosine], 1)], 0)
    return (forward.astype(jnp.bfloat16), backward.astype(jnp.bfloat16))

def measure(raw_counts, resample_delta):
    points = resample_delta.shape[0]
    resample = (jnp.eye(points, dtype=jnp.float32) + resample_delta).astype(jnp.bfloat16)
    first = jnp.einsum('ij,kjl->kil', resample.astype(jnp.float32), raw_counts.astype(jnp.float32)).astype(jnp.bfloat16)
    second = jnp.einsum('kij,lj->kil', first.astype(jnp.float32), resample.astype(jnp.float32))
    return jnp.sqrt(jnp.maximum(second, 0.0)).astype(jnp.bfloat16)

def frame_terms(window, probe, amplitude, forward, backward):
    mode_count = probe.shape[0]
    points = probe.shape[-1]
    probe_real = probe[:, 0]
    probe_imag = probe[:, 1]
    object_real = window[0]
    object_imag = window[1]
    wave = jnp.stack([probe_real * object_real - probe_imag * object_imag, probe_real * object_imag + probe_imag * object_real], 1)
    wave_cols = wave.transpose(1, 2, 0, 3).reshape(2 * points, mode_count * points).astype(jnp.bfloat16)
    half_done = product(forward, wave_cols).astype(jnp.bfloat16)
    wave_rows = half_done.reshape(2, points, mode_count, points).transpose(2, 1, 0, 3).reshape(mode_count * points, 2 * points)
    far_field = product(wave_rows, backward).reshape(mode_count, points, 2, points)
    intensity = lax.optimization_barrier(jnp.sum(far_field * far_field, axis=(0, 2)))
    scaling = 1.0 - amplitude.astype(jnp.float32) / jnp.sqrt(jnp.maximum(intensity, 1.0))
    residual = (far_field * scaling[None, :, None, :]).astype(jnp.bfloat16).reshape(mode_count * points, 2 * points)
    back_rows = product(residual, forward).astype(jnp.bfloat16)
    back_cols = back_rows.reshape(mode_count, points, 2, points).transpose(2, 1, 0, 3).reshape(2 * points, mode_count * points)
    update = product(backward, back_cols).reshape(2, points, mode_count, points).transpose(2, 0, 1, 3)
    update_real = update[:, 0]
    update_imag = update[:, 1]
    object_term = jnp.stack([lax.optimization_barrier(jnp.sum(probe_real * update_real + probe_imag * update_imag, 0)), lax.optimization_barrier(jnp.sum(probe_real * update_imag - probe_imag * update_real, 0))], 0)
    probe_term = jnp.stack([object_real * update_real + object_imag * update_imag, object_real * update_imag - object_imag * update_real], 1)
    return (object_term, probe_term)

def reference(object_field, probe, raw_counts, resample_delta, tile_row, offsets):
    points = probe.shape[-1]
    half = points // 2
    forward, backward = dft_tables(points)
    amplitudes = measure(raw_counts, resample_delta)
    padded = jnp.pad(object_field, ((0, 0), (half, half), (half, half)))
    frame_ids = jnp.arange(FRAMES, dtype=jnp.int32)
    tile_cols = frame_ids // FR_DEV % N_COL
    tops = (tile_row[:, 0] * TILE + offsets[:, 0]).astype(jnp.int32)
    lefts = (tile_cols * TILE + offsets[:, 1]).astype(jnp.int32)
    anchor = jnp.zeros((), jnp.int32)

    def one_frame(totals, inputs):
        gradient, probe_total = totals
        amplitude, top, left = inputs
        window = lax.dynamic_slice(padded, (anchor, top, left), (2, points, points))
        object_term, probe_term = frame_terms(window, probe, amplitude, forward, backward)
        current = lax.dynamic_slice(gradient, (anchor, top, left), (2, points, points))
        gradient = lax.dynamic_update_slice(gradient, current + object_term, (anchor, top, left))
        return ((gradient, probe_total + probe_term), None)
    start = (jnp.zeros(padded.shape, padded.dtype), jnp.zeros(probe.shape, probe.dtype))
    (gradient, probe_total), _ = lax.scan(one_frame, start, (amplitudes, tops, lefts))
    object_grad = gradient[:, half:half + OBJ_ROWS, half:half + OBJ_COLS]
    probe_grad = probe_total * (1.0 / math.sqrt(FRAMES))
    return (object_grad, probe_grad)
```

```python
import functools
import math

import jax
import jax.numpy as jnp
from jax import lax
from jax.experimental import pallas as pl
from jax.experimental.pallas import tpu as pltpu
from jax.sharding import Mesh
from jax.sharding import PartitionSpec as P

ROW = ("row_0", "row_1", "row_2")
ROW_COL = ("row_0", "row_1", "row_2", "col")
AROUND = ((-1, -1), (-1, 0), (-1, 1), (0, -1), (0, 1), (1, -1), (1, 0), (1, 1))
VMEM_BYTES = 56 * 2**20


def dft_tables(points):
    indices = jnp.arange(points, dtype=jnp.int32)
    phases = indices[:, None] * indices[None, :] % points
    angles = phases.astype(jnp.float32) * (2.0 * math.pi / points)
    norming = 1.0 / math.sqrt(points)
    cosine = jnp.cos(angles) * norming
    sine_part = -jnp.sin(angles) * norming
    forward = jnp.concatenate(
        [jnp.concatenate([cosine, -sine_part], 1), jnp.concatenate([sine_part, cosine], 1)], 0
    )
    backward = jnp.concatenate(
        [jnp.concatenate([cosine, sine_part], 1), jnp.concatenate([-sine_part, cosine], 1)], 0
    )
    return (forward.astype(jnp.bfloat16), backward.astype(jnp.bfloat16))


def spread_kernel(target, counts, slots, sems):
    copies = [
        pltpu.make_async_copy(counts.at[j], slots.at[target[j]], sems.at[j]) for j in range(counts.shape[0])
    ]
    for copy in copies:
        copy.start()
    for copy in copies:
        copy.wait()


def spread(target, counts, slot_count):
    return pl.pallas_call(
        spread_kernel,
        grid_spec=pltpu.PrefetchScalarGridSpec(
            num_scalar_prefetch=1,
            grid=(1,),
            in_specs=[pl.BlockSpec(memory_space=pl.ANY)],
            out_specs=pl.BlockSpec(memory_space=pl.ANY),
            scratch_shapes=[pltpu.SemaphoreType.DMA((counts.shape[0],))],
        ),
        out_shape=jax.ShapeDtypeStruct((slot_count,) + counts.shape[1:], counts.dtype),
        name="spread",
    )(target, counts)


def regions(half, tile):
    span = {-1: (0, half), 0: (half, tile), 1: (half + tile, half)}
    return [span[a] + span[b] for a, b in ((0, 0),) + AROUND]


def frames_kernel(order, count, tops, lefts, raw, probe, fwd, bwd, res, res_t, *refs, points, modes, spots):
    pieces, (pgrad, *grads) = refs[:9], refs[9:19]
    ext, grad, win, stack, rows, field, update, amp, sems = refs[19:]
    n = points
    tiles = n // 128
    i = pl.program_id(0)

    @pl.when(i == 0)
    def _():
        copies = [
            pltpu.make_async_copy(piece, ext.at[:, pl.ds(r, h), pl.ds(c, w)], sems.at[k])
            for k, (piece, (r, h, c, w)) in enumerate(zip(pieces, spots))
        ]
        for copy in copies:
            copy.start()
        grad[...] = jnp.zeros(grad.shape, jnp.float32)
        pgrad[...] = jnp.zeros(pgrad.shape, jnp.float32)
        for copy in copies:
            copy.wait()

    def dot(x, y):
        return jnp.dot(x, y, preferred_element_type=jnp.float32)

    @pl.when(i < count[0])
    def _():
        slot = order[i]
        top = tops[slot]
        left = lefts[slot]
        base = pl.multiple_of(left // 128 * 128, 128)
        shift = left - base
        back = lax.rem(128 - shift, 128)
        floor = pl.multiple_of(top // 8 * 8, 8)
        low = top - floor
        up = lax.rem(8 - low, 8)
        lane = lax.broadcasted_iota(jnp.int32, (8, 128), 1)
        sub = lax.broadcasted_iota(jnp.int32, (8, 128), 0)
        keep = lane < 128 - shift
        upper = sub < 8 - low

        def strip(part, g):
            cols = [
                pltpu.roll(ext[part, pl.ds(floor + 8 * g, 8), pl.ds(base + 128 * j, 128)], back, 1)
                for j in range(tiles + 1)
            ]
            vals = [jnp.where(keep, cols[j], cols[j + 1]) for j in range(tiles)]
            return [pltpu.roll(v, up, 0) for v in vals]

        prev = [strip(part, 0) for part in range(2)]
        for k in range(n // 16):
            halves = []
            for h in range(2):
                following = [strip(part, 2 * k + h + 1) for part in range(2)]
                halves.append(
                    [
                        [jnp.where(upper, prev[part][j], following[part][j]) for j in range(tiles)]
                        for part in range(2)
                    ]
                )
                prev = following
            obj = [
                jnp.concatenate([jnp.concatenate(halves[h][part], 1) for h in range(2)], 0)
                for part in range(2)
            ]
            r = 16 * k
            for part in range(2):
                win[part, r : r + 16, :] = obj[part]
            for m in range(modes):
                p_re = probe[m, 0, r : r + 16, :]
                p_im = probe[m, 1, r : r + 16, :]
                psi_re = (p_re * obj[0] - p_im * obj[1]).astype(jnp.bfloat16)
                psi_im = (p_re * obj[1] + p_im * obj[0]).astype(jnp.bfloat16)
                stack[r : r + 16, m * n : (m + 1) * n] = psi_re
                stack[n + r : n + r + 16, m * n : (m + 1) * n] = psi_im
        first = dot(res[...], raw[0]).astype(jnp.bfloat16)
        second = dot(first, res_t[...])
        amp[...] = jnp.sqrt(jnp.maximum(second, 0.0)).astype(jnp.bfloat16).astype(jnp.float32)
        for m in range(modes):
            half_done = dot(fwd[...], stack[:, m * n : (m + 1) * n]).astype(jnp.bfloat16)
            rows[m * n : (m + 1) * n, 0:n] = half_done[:n]
            rows[m * n : (m + 1) * n, n : 2 * n] = half_done[n:]
        field[...] = dot(rows[...], bwd[...])
        for k in range(n // 8):
            r = 8 * k
            far = [field[m * n + r : m * n + r + 8, :] for m in range(modes)]
            total = far[0] * far[0]
            for m in range(1, modes):
                total = total + far[m] * far[m]
            total = total[:, :n] + total[:, n:]
            scaling = 1.0 - amp[r : r + 8, :] * lax.rsqrt(jnp.maximum(total, 1.0))
            scaling = jnp.concatenate([scaling, scaling], 1)
            for m in range(modes):
                rows[m * n + r : m * n + r + 8, :] = (far[m] * scaling).astype(jnp.bfloat16)
        for m in range(modes):
            turned = dot(rows[m * n : (m + 1) * n, :], fwd[...]).astype(jnp.bfloat16)
            stack[0:n, m * n : (m + 1) * n] = turned[:, :n]
            stack[n : 2 * n, m * n : (m + 1) * n] = turned[:, n:]
        update[...] = dot(bwd[...], stack[...])
        fresh = lane >= shift
        lower = sub >= low
        zero = jnp.zeros((8, 128), jnp.float32)
        last = [[zero] * tiles, [zero] * tiles]
        for g in range(n // 8 + 1):
            r = 8 * g
            if g < n // 8:
                o_re = win[0, r : r + 8, :]
                o_im = win[1, r : r + 8, :]
                t_re = t_im = None
                for m in range(modes):
                    u_re = update[r : r + 8, m * n : (m + 1) * n]
                    u_im = update[n + r : n + r + 8, m * n : (m + 1) * n]
                    p_re = probe[m, 0, r : r + 8, :]
                    p_im = probe[m, 1, r : r + 8, :]
                    a_re = p_re * u_re + p_im * u_im
                    a_im = p_re * u_im - p_im * u_re
                    t_re = a_re if t_re is None else t_re + a_re
                    t_im = a_im if t_im is None else t_im + a_im
                    pgrad[m, 0, r : r + 8, :] += o_re * u_re + o_im * u_im
                    pgrad[m, 1, r : r + 8, :] += o_re * u_im - o_im * u_re
                terms = [
                    [pltpu.roll(t[:, 128 * j : 128 * (j + 1)], low, 0) for j in range(tiles)]
                    for t in (t_re, t_im)
                ]
            else:
                terms = [[zero] * tiles, [zero] * tiles]
            for part in range(2):
                placed = [jnp.where(lower, terms[part][j], last[part][j]) for j in range(tiles)]
                turned = [zero] + [pltpu.roll(v, shift, 1) for v in placed] + [zero]
                for j in range(tiles + 1):
                    block = jnp.where(fresh, turned[j + 1], turned[j])
                    grad[part, pl.ds(floor + r, 8), pl.ds(base + 128 * j, 128)] += block
            last = terms

    @pl.when(i == pl.num_programs(0) - 1)
    def _():
        copies = [
            pltpu.make_async_copy(grad.at[:, pl.ds(r, h), pl.ds(c, w)], piece, sems.at[k])
            for k, (piece, (r, h, c, w)) in enumerate(zip(grads, spots))
        ]
        for copy in copies:
            copy.start()
        for copy in copies:
            copy.wait()


def run_frames(order, count, tops, lefts, raw, probe, fwd, bwd, res, res_t, pieces, half, tile):
    modes, _, n, _ = probe.shape
    spots = regions(half, tile)
    wide = tile + 2 * half
    anywhere = pl.BlockSpec(memory_space=pl.ANY)

    def whole(a):
        return pl.BlockSpec(a.shape, lambda i, *_: (0,) * a.ndim, pipeline_mode=pl.Buffered(1))

    outs = [jax.ShapeDtypeStruct(probe.shape, jnp.float32)]
    outs += [jax.ShapeDtypeStruct((2, h, w), jnp.float32) for _, h, _, w in spots]
    spec = pltpu.PrefetchScalarGridSpec(
        num_scalar_prefetch=4,
        grid=(raw.shape[0],),
        in_specs=[pl.BlockSpec((1, n, n), lambda i, order, *_: (order[i], 0, 0))]
        + [whole(a) for a in (probe, fwd, bwd, res, res_t)]
        + [anywhere] * 9,
        out_specs=[whole(outs[0])] + [anywhere] * 9,
        scratch_shapes=[
            pltpu.VMEM((2, wide, wide), jnp.float32),
            pltpu.VMEM((2, wide, wide), jnp.float32),
            pltpu.VMEM((2, n, n), jnp.float32),
            pltpu.VMEM((2 * n, modes * n), jnp.bfloat16),
            pltpu.VMEM((modes * n, 2 * n), jnp.bfloat16),
            pltpu.VMEM((modes * n, 2 * n), jnp.float32),
            pltpu.VMEM((2 * n, modes * n), jnp.float32),
            pltpu.VMEM((n, n), jnp.float32),
            pltpu.SemaphoreType.DMA((9,)),
        ],
    )
    return pl.pallas_call(
        functools.partial(frames_kernel, points=n, modes=modes, spots=spots),
        grid_spec=spec,
        out_shape=outs,
        compiler_params=pltpu.CompilerParams(
            dimension_semantics=("arbitrary",), vmem_limit_bytes=VMEM_BYTES
        ),
        name="frames",
    )(order, count, tops, lefts, raw, probe, fwd, bwd, res, res_t, *pieces)


def to_neighbour(value, step):
    rows, cols = lax.axis_size(ROW), lax.axis_size("col")
    pairs = [
        (r * cols + c, (r + step[0]) * cols + c + step[1])
        for r in range(rows)
        for c in range(cols)
        if 0 <= r + step[0] < rows and 0 <= c + step[1] < cols
    ]
    return lax.ppermute(value, ROW_COL, pairs)


def edge(value, step, width):
    for dim, s in ((1, step[0]), (2, step[1])):
        length = value.shape[dim]
        if s < 0:
            value = lax.slice_in_dim(value, 0, width, axis=dim)
        elif s > 0:
            value = lax.slice_in_dim(value, length - width, length, axis=dim)
    return value


def merge_kernel(own, *refs, half, tile):
    out = refs[-1]
    out[...] = own[...]
    span = {-1: (0, half), 0: (0, tile), 1: (tile - half, tile)}
    for piece, (a, b) in zip(refs[:-1], AROUND):
        (r0, r1), (c0, c1) = span[a], span[b]
        out[:, r0:r1, c0:c1] += piece[...]


def merge(own, pieces, half):
    def block(a):
        return pl.BlockSpec((1,) + a.shape[1:], lambda i: (i, 0, 0))

    return pl.pallas_call(
        functools.partial(merge_kernel, half=half, tile=own.shape[1]),
        grid=(own.shape[0],),
        in_specs=[block(own)] + [block(p) for p in pieces],
        out_specs=block(own),
        out_shape=jax.ShapeDtypeStruct(own.shape, own.dtype),
        compiler_params=pltpu.CompilerParams(
            dimension_semantics=("arbitrary",), vmem_limit_bytes=VMEM_BYTES
        ),
        name="merge",
    )(own, *pieces)


def sum_over_devices(value, halved, whole, scale):
    taken = []
    for axis, bit in halved:
        size = lax.axis_size(axis)
        side = lax.axis_index(axis) // bit % 2
        pairs = [(j, j ^ bit) for j in range(size)]
        length = value.shape[0] // 2
        mine = lax.dynamic_slice_in_dim(value, side * length, length, 0)
        other = lax.dynamic_slice_in_dim(value, (1 - side) * length, length, 0)
        value = mine + lax.ppermute(other, axis, pairs)
        taken.append((axis, pairs, side))
    for axis, bit in whole:
        pairs = [(j, j ^ bit) for j in range(lax.axis_size(axis))]
        value = value + lax.ppermute(value, axis, pairs)
    value = value * scale
    for axis, pairs, side in reversed(taken):
        other = lax.ppermute(value, axis, pairs)
        value = jnp.where(
            side == 0, jnp.concatenate([value, other], 0), jnp.concatenate([other, value], 0)
        )
    return value


def shards(object_field, probe, raw_counts, resample_delta, tile_row, offsets):
    modes, _, points, _ = probe.shape
    half = points // 2
    tile = object_field.shape[1]
    tile_rows = lax.axis_size(ROW)
    frame_total = raw_counts.shape[0] * tile_rows * lax.axis_size("col")
    target = tile_row[:, 0]
    slots = spread(target, raw_counts, tile_rows)
    slot_ids = jnp.arange(tile_rows, dtype=jnp.int32)
    picks = (target[:, None] == slot_ids[None, :]).astype(jnp.int32)
    requests = jnp.stack(
        [jnp.sum(picks * offsets[:, 0:1], 0), jnp.sum(picks * offsets[:, 1:2], 0), jnp.sum(picks, 0)], 1
    )
    received = lax.all_to_all(requests, ROW, split_axis=0, concat_axis=0, tiled=True)
    arrived = lax.all_to_all(slots, ROW, split_axis=0, concat_axis=0, tiled=True)
    around = [to_neighbour(edge(object_field, (-a, -b), half), (-a, -b)) for a, b in AROUND]
    live = received[:, 2]
    count = jnp.sum(live)
    rank = jnp.sum(jnp.where(slot_ids[None, :] < slot_ids[:, None], live[None, :], 0), 1)
    place = jnp.minimum(slot_ids, jnp.maximum(count - 1, 0))
    hit = (rank[None, :] == place[:, None]) & (live[None, :] > 0)
    order = jnp.sum(jnp.where(hit, slot_ids[None, :], 0), 1)
    forward, backward = dft_tables(points)
    resample = (jnp.eye(points, dtype=jnp.float32) + resample_delta).astype(jnp.bfloat16)
    probe_total, own, *outer = run_frames(
        order, count[None], received[:, 0], received[:, 1], arrived, probe, forward, backward,
        resample, resample.T, [object_field] + around, half, tile,
    )
    halved = (("row_2", 1), ("col", 1), ("col", 2))
    whole = (("col", 4), ("row_1", 1), ("row_0", 1), ("row_0", 2))
    probe_grad = sum_over_devices(
        probe_total.reshape(-1, points), halved, whole, 1.0 / math.sqrt(frame_total)
    ).reshape(probe.shape)
    inward = [to_neighbour(piece, step) for piece, step in zip(outer, AROUND)]
    back = [inward[AROUND.index((-a, -b))] for a, b in AROUND]
    object_grad = merge(own, back, half)
    return (object_grad, probe_grad)


def solution(mesh):
    torus = Mesh(
        mesh.devices.reshape(4, 2, 2, mesh.shape["col"]), ("row_0", "row_1", "row_2", "col")
    )
    return jax.shard_map(
        shards,
        mesh=torus,
        in_specs=(
            P(None, ROW, "col"),
            P(),
            P(ROW_COL, None, None),
            P(),
            P(ROW_COL, None),
            P(ROW_COL, None),
        ),
        out_specs=(P(None, ROW, "col"), P()),
        check_vma=False,
    )
```

```python
import functools
import math

import jax
import jax.numpy as jnp
from jax import lax
from jax.experimental import pallas as pl
from jax.experimental.pallas import tpu as pltpu
from jax.sharding import Mesh
from jax.sharding import PartitionSpec as P

ROW = ("row_0", "row_1", "row_2")
ROW_COL = ("row_0", "row_1", "row_2", "col")
AROUND = ((-1, -1), (-1, 0), (-1, 1), (0, -1), (0, 1), (1, -1), (1, 0), (1, 1))
VMEM_BYTES = 56 * 2**20


def dft_tables(points):
    indices = jnp.arange(points, dtype=jnp.int32)
    phases = indices[:, None] * indices[None, :] % points
    angles = phases.astype(jnp.float32) * (2.0 * math.pi / points)
    norming = 1.0 / math.sqrt(points)
    cosine = jnp.cos(angles) * norming
    sine_part = -jnp.sin(angles) * norming
    forward = jnp.concatenate(
        [jnp.concatenate([cosine, -sine_part], 1), jnp.concatenate([sine_part, cosine], 1)], 0
    )
    backward = jnp.concatenate(
        [jnp.concatenate([cosine, sine_part], 1), jnp.concatenate([-sine_part, cosine], 1)], 0
    )
    return (forward.astype(jnp.bfloat16), backward.astype(jnp.bfloat16))


def spread_kernel(target, frame, slot):
    slot[...] = frame[...]


def spread(target, counts, slot_count):
    block = (1,) + counts.shape[1:]
    return pl.pallas_call(
        spread_kernel,
        grid_spec=pltpu.PrefetchScalarGridSpec(
            num_scalar_prefetch=1,
            grid=(counts.shape[0],),
            in_specs=[pl.BlockSpec(block, lambda j, target: (j, 0, 0))],
            out_specs=pl.BlockSpec(block, lambda j, target: (target[j], 0, 0)),
        ),
        out_shape=jax.ShapeDtypeStruct((slot_count,) + counts.shape[1:], counts.dtype),
        name="spread",
    )(target, counts)


def regions(half, tile):
    span = {-1: (0, half), 0: (half, tile), 1: (half + tile, half)}
    return [span[a] + span[b] for a, b in ((0, 0),) + AROUND]


def frames_kernel(order, count, tops, lefts, raw, probe, fwd, bwd, res, res_t, *refs, points, modes, spots):
    pieces, (pgrad, *grads) = refs[:9], refs[9:19]
    ext, grad, win, stack, rows, field, update, amp, sems = refs[19:]
    n = points
    tiles = n // 128
    i = pl.program_id(0)

    @pl.when(i == 0)
    def _():
        copies = [
            pltpu.make_async_copy(piece, ext.at[:, pl.ds(r, h), pl.ds(c, w)], sems.at[k])
            for k, (piece, (r, h, c, w)) in enumerate(zip(pieces, spots))
        ]
        for copy in copies:
            copy.start()
        grad[...] = jnp.zeros(grad.shape, jnp.float32)
        pgrad[...] = jnp.zeros(pgrad.shape, jnp.float32)
        for copy in copies:
            copy.wait()

    def dot(x, y):
        return jnp.dot(x, y, preferred_element_type=jnp.float32)

    @pl.when(i < count[0])
    def _():
        slot = order[i]
        top = tops[slot]
        left = lefts[slot]
        base = pl.multiple_of(left // 128 * 128, 128)
        shift = left - base
        back = lax.rem(128 - shift, 128)
        floor = pl.multiple_of(top // 8 * 8, 8)
        low = top - floor
        up = lax.rem(8 - low, 8)
        lane = lax.broadcasted_iota(jnp.int32, (8, 128), 1)
        sub = lax.broadcasted_iota(jnp.int32, (8, 128), 0)
        keep = lane < 128 - shift
        upper = sub < 8 - low

        def strip(part, g):
            cols = [
                pltpu.roll(ext[part, pl.ds(floor + 8 * g, 8), pl.ds(base + 128 * j, 128)], back, 1)
                for j in range(tiles + 1)
            ]
            vals = [jnp.where(keep, cols[j], cols[j + 1]) for j in range(tiles)]
            return [pltpu.roll(v, up, 0) for v in vals]

        prev = [strip(part, 0) for part in range(2)]
        for k in range(n // 16):
            halves = []
            for h in range(2):
                following = [strip(part, 2 * k + h + 1) for part in range(2)]
                halves.append(
                    [
                        [jnp.where(upper, prev[part][j], following[part][j]) for j in range(tiles)]
                        for part in range(2)
                    ]
                )
                prev = following
            obj = [
                jnp.concatenate([jnp.concatenate(halves[h][part], 1) for h in range(2)], 0)
                for part in range(2)
            ]
            r = 16 * k
            for part in range(2):
                win[part, r : r + 16, :] = obj[part]
            for m in range(modes):
                p_re = probe[m, 0, r : r + 16, :]
                p_im = probe[m, 1, r : r + 16, :]
                psi_re = (p_re * obj[0] - p_im * obj[1]).astype(jnp.bfloat16)
                psi_im = (p_re * obj[1] + p_im * obj[0]).astype(jnp.bfloat16)
                stack[r : r + 16, m * n : (m + 1) * n] = psi_re
                stack[n + r : n + r + 16, m * n : (m + 1) * n] = psi_im
        first = dot(res[...], raw[0]).astype(jnp.bfloat16)
        second = dot(first, res_t[...])
        amp[...] = jnp.sqrt(jnp.maximum(second, 0.0)).astype(jnp.bfloat16).astype(jnp.float32)
        for m in range(modes):
            half_done = dot(fwd[...], stack[:, m * n : (m + 1) * n]).astype(jnp.bfloat16)
            rows[m * n : (m + 1) * n, 0:n] = half_done[:n]
            rows[m * n : (m + 1) * n, n : 2 * n] = half_done[n:]
        field[...] = dot(rows[...], bwd[...])
        for k in range(n // 8):
            r = 8 * k
            far = [field[m * n + r : m * n + r + 8, :] for m in range(modes)]
            total = far[0] * far[0]
            for m in range(1, modes):
                total = total + far[m] * far[m]
            total = total[:, :n] + total[:, n:]
            scaling = 1.0 - amp[r : r + 8, :] * lax.rsqrt(jnp.maximum(total, 1.0))
            scaling = jnp.concatenate([scaling, scaling], 1)
            for m in range(modes):
                rows[m * n + r : m * n + r + 8, :] = (far[m] * scaling).astype(jnp.bfloat16)
        for m in range(modes):
            turned = dot(rows[m * n : (m + 1) * n, :], fwd[...]).astype(jnp.bfloat16)
            stack[0:n, m * n : (m + 1) * n] = turned[:, :n]
            stack[n : 2 * n, m * n : (m + 1) * n] = turned[:, n:]
        update[...] = dot(bwd[...], stack[...])
        fresh = lane >= shift
        lower = sub >= low
        zero = jnp.zeros((8, 128), jnp.float32)
        last = [[zero] * tiles, [zero] * tiles]
        for g in range(n // 8 + 1):
            r = 8 * g
            if g < n // 8:
                o_re = win[0, r : r + 8, :]
                o_im = win[1, r : r + 8, :]
                t_re = t_im = None
                for m in range(modes):
                    u_re = update[r : r + 8, m * n : (m + 1) * n]
                    u_im = update[n + r : n + r + 8, m * n : (m + 1) * n]
                    p_re = probe[m, 0, r : r + 8, :]
                    p_im = probe[m, 1, r : r + 8, :]
                    a_re = p_re * u_re + p_im * u_im
                    a_im = p_re * u_im - p_im * u_re
                    t_re = a_re if t_re is None else t_re + a_re
                    t_im = a_im if t_im is None else t_im + a_im
                    pgrad[m, 0, r : r + 8, :] += o_re * u_re + o_im * u_im
                    pgrad[m, 1, r : r + 8, :] += o_re * u_im - o_im * u_re
                terms = [
                    [pltpu.roll(t[:, 128 * j : 128 * (j + 1)], low, 0) for j in range(tiles)]
                    for t in (t_re, t_im)
                ]
            else:
                terms = [[zero] * tiles, [zero] * tiles]
            for part in range(2):
                placed = [jnp.where(lower, terms[part][j], last[part][j]) for j in range(tiles)]
                turned = [zero] + [pltpu.roll(v, shift, 1) for v in placed] + [zero]
                for j in range(tiles + 1):
                    block = jnp.where(fresh, turned[j + 1], turned[j])
                    grad[part, pl.ds(floor + r, 8), pl.ds(base + 128 * j, 128)] += block
            last = terms

    @pl.when(i == pl.num_programs(0) - 1)
    def _():
        copies = [
            pltpu.make_async_copy(grad.at[:, pl.ds(r, h), pl.ds(c, w)], piece, sems.at[k])
            for k, (piece, (r, h, c, w)) in enumerate(zip(grads, spots))
        ]
        for copy in copies:
            copy.start()
        for copy in copies:
            copy.wait()


def run_frames(order, count, tops, lefts, raw, probe, fwd, bwd, res, res_t, pieces, half, tile):
    modes, _, n, _ = probe.shape
    spots = regions(half, tile)
    wide = tile + 2 * half
    anywhere = pl.BlockSpec(memory_space=pl.ANY)

    def whole(a):
        return pl.BlockSpec(a.shape, lambda i, *_: (0,) * a.ndim, pipeline_mode=pl.Buffered(1))

    outs = [jax.ShapeDtypeStruct(probe.shape, jnp.float32)]
    outs += [jax.ShapeDtypeStruct((2, h, w), jnp.float32) for _, h, _, w in spots]
    spec = pltpu.PrefetchScalarGridSpec(
        num_scalar_prefetch=4,
        grid=(raw.shape[0],),
        in_specs=[pl.BlockSpec((1, n, n), lambda i, order, *_: (order[i], 0, 0))]
        + [whole(a) for a in (probe, fwd, bwd, res, res_t)]
        + [anywhere] * 9,
        out_specs=[whole(outs[0])] + [anywhere] * 9,
        scratch_shapes=[
            pltpu.VMEM((2, wide, wide), jnp.float32),
            pltpu.VMEM((2, wide, wide), jnp.float32),
            pltpu.VMEM((2, n, n), jnp.float32),
            pltpu.VMEM((2 * n, modes * n), jnp.bfloat16),
            pltpu.VMEM((modes * n, 2 * n), jnp.bfloat16),
            pltpu.VMEM((modes * n, 2 * n), jnp.float32),
            pltpu.VMEM((2 * n, modes * n), jnp.float32),
            pltpu.VMEM((n, n), jnp.float32),
            pltpu.SemaphoreType.DMA((9,)),
        ],
    )
    return pl.pallas_call(
        functools.partial(frames_kernel, points=n, modes=modes, spots=spots),
        grid_spec=spec,
        out_shape=outs,
        compiler_params=pltpu.CompilerParams(
            dimension_semantics=("arbitrary",), vmem_limit_bytes=VMEM_BYTES
        ),
        name="frames",
    )(order, count, tops, lefts, raw, probe, fwd, bwd, res, res_t, *pieces)


def to_neighbour(value, step):
    rows, cols = lax.axis_size(ROW), lax.axis_size("col")
    pairs = [
        (r * cols + c, (r + step[0]) * cols + c + step[1])
        for r in range(rows)
        for c in range(cols)
        if 0 <= r + step[0] < rows and 0 <= c + step[1] < cols
    ]
    return lax.ppermute(value, ROW_COL, pairs)


def edge(value, step, width):
    for dim, s in ((1, step[0]), (2, step[1])):
        length = value.shape[dim]
        if s < 0:
            value = lax.slice_in_dim(value, 0, width, axis=dim)
        elif s > 0:
            value = lax.slice_in_dim(value, length - width, length, axis=dim)
    return value


def merge_kernel(own, *refs, half, tile):
    out = refs[-1]
    out[...] = own[...]
    span = {-1: (0, half), 0: (0, tile), 1: (tile - half, tile)}
    for piece, (a, b) in zip(refs[:-1], AROUND):
        (r0, r1), (c0, c1) = span[a], span[b]
        out[:, r0:r1, c0:c1] += piece[...]


def merge(own, pieces, half):
    def block(a):
        return pl.BlockSpec((1,) + a.shape[1:], lambda i: (i, 0, 0))

    return pl.pallas_call(
        functools.partial(merge_kernel, half=half, tile=own.shape[1]),
        grid=(own.shape[0],),
        in_specs=[block(own)] + [block(p) for p in pieces],
        out_specs=block(own),
        out_shape=jax.ShapeDtypeStruct(own.shape, own.dtype),
        compiler_params=pltpu.CompilerParams(
            dimension_semantics=("arbitrary",), vmem_limit_bytes=VMEM_BYTES
        ),
        name="merge",
    )(own, *pieces)


def exchanged(values, axis, bit):
    pairs = [(j, j ^ bit) for j in range(lax.axis_size(axis))]
    return [lax.ppermute(value, axis, pairs) for value in values]


def sum_over_devices(value, first, halved, whole, scale, meanwhile):
    def side(axis, bit):
        return lax.axis_index(axis) // bit % 2

    def split(v, axis, bit):
        length = v.shape[0] // 2
        s = side(axis, bit)
        mine = lax.dynamic_slice_in_dim(v, s * length, length, 0)
        other = lax.dynamic_slice_in_dim(v, (1 - s) * length, length, 0)
        return mine + exchanged([other], axis, bit)[0]

    def joined(v, axis, bit):
        other = exchanged([v], axis, bit)[0]
        return jnp.where(
            side(axis, bit) == 0, jnp.concatenate([v, other], 0), jnp.concatenate([other, v], 0)
        )

    value = split(value, *first)
    cut = value.shape[0] // 2
    chains = [value[:cut], value[cut:]]
    for step in range(len(halved[0])):
        chains = [split(v, *halved[k][step]) for k, v in enumerate(chains)]
    for step in range(len(whole[0])):
        chains = [v + exchanged([v], *whole[k][step])[0] for k, v in enumerate(chains)]
        if step == 0:
            chains, meanwhile = lax.optimization_barrier((chains, meanwhile))
    chains = [v * scale for v in chains]
    for step in reversed(range(len(halved[0]))):
        chains = [joined(v, *halved[k][step]) for k, v in enumerate(chains)]
    return joined(jnp.concatenate(chains, 0), *first), meanwhile


def shards(object_field, probe, raw_counts, resample_delta, tile_row, offsets):
    modes, _, points, _ = probe.shape
    half = points // 2
    tile = object_field.shape[1]
    tile_rows = lax.axis_size(ROW)
    frame_total = raw_counts.shape[0] * tile_rows * lax.axis_size("col")
    target = tile_row[:, 0]
    slots = spread(target, raw_counts, tile_rows)
    slot_ids = jnp.arange(tile_rows, dtype=jnp.int32)
    picks = (target[:, None] == slot_ids[None, :]).astype(jnp.int32)
    requests = jnp.stack(
        [jnp.sum(picks * offsets[:, 0:1], 0), jnp.sum(picks * offsets[:, 1:2], 0), jnp.sum(picks, 0)], 1
    )
    received = lax.all_to_all(requests, ROW, split_axis=0, concat_axis=0, tiled=True)
    arrived = lax.all_to_all(slots, ROW, split_axis=0, concat_axis=0, tiled=True)
    around = [to_neighbour(edge(object_field, (-a, -b), half), (-a, -b)) for a, b in AROUND]
    live = received[:, 2]
    count = jnp.sum(live)
    rank = jnp.sum(jnp.where(slot_ids[None, :] < slot_ids[:, None], live[None, :], 0), 1)
    place = jnp.minimum(slot_ids, jnp.maximum(count - 1, 0))
    hit = (rank[None, :] == place[:, None]) & (live[None, :] > 0)
    order = jnp.sum(jnp.where(hit, slot_ids[None, :], 0), 1)
    forward, backward = dft_tables(points)
    resample = (jnp.eye(points, dtype=jnp.float32) + resample_delta).astype(jnp.bfloat16)
    probe_total, own, *outer = run_frames(
        order, count[None], received[:, 0], received[:, 1], arrived, probe, forward, backward,
        resample, resample.T, [object_field] + around, half, tile,
    )
    inward = [to_neighbour(piece, step) for piece, step in zip(outer, AROUND)]
    x, z = ("row_0", 1), ("col", 2)
    rest = (("row_0", 2), ("col", 4), ("col", 1), ("row_1", 1))
    probe_grad, inward = sum_over_devices(
        probe_total.reshape(-1, points), ("row_2", 1), ((x, z), (z, x)), (rest, rest[1::-1] + rest[2:]),
        1.0 / math.sqrt(frame_total), inward,
    )
    probe_grad = probe_grad.reshape(probe.shape)
    back = [inward[AROUND.index((-a, -b))] for a, b in AROUND]
    object_grad = merge(own, back, half)
    return (object_grad, probe_grad)


def solution(mesh):
    torus = Mesh(
        mesh.devices.reshape(4, 2, 2, mesh.shape["col"]), ("row_0", "row_1", "row_2", "col")
    )
    return jax.shard_map(
        shards,
        mesh=torus,
        in_specs=(
            P(None, ROW, "col"),
            P(),
            P(ROW_COL, None, None),
            P(),
            P(ROW_COL, None),
            P(ROW_COL, None),
        ),
        out_specs=(P(None, ROW, "col"), P()),
        check_vma=False,
    )
```

```python
import functools
import math

import jax
import jax.numpy as jnp
from jax import lax
from jax.experimental import pallas as pl
from jax.experimental.pallas import tpu as pltpu
from jax.sharding import Mesh
from jax.sharding import PartitionSpec as P

ROW = ("x", "y_far", "core")
COL = ("z", "y_near")
ROW_COL = ROW + COL
VMEM_BYTES = 52 * 2**20
HEADROOM = 14.0
NOTE_ROWS = 16


def dft_table(left, right, points, sign):
    phases = left[:, None] * right[None, :] % points
    angles = phases.astype(jnp.float32) * (2.0 * math.pi / points)
    norming = 1.0 / math.sqrt(points)
    cosine = jnp.cos(angles) * norming
    sine_part = -jnp.sin(angles) * norming * sign
    table = jnp.concatenate(
        [jnp.concatenate([cosine, -sine_part], 1), jnp.concatenate([sine_part, cosine], 1)], 0
    )
    return table.astype(jnp.bfloat16)


def spread_kernel(target, counts, slots, held, sems):
    count = counts.shape[0]
    inward = [pltpu.make_async_copy(counts.at[j], held.at[j], sems.at[0, j]) for j in range(count)]
    outward = [pltpu.make_async_copy(held.at[j], slots.at[target[j]], sems.at[1, j]) for j in range(count)]
    for copy in inward:
        copy.start()
    for j in range(count):
        inward[j].wait()
        outward[j].start()
    for copy in outward:
        copy.wait()


def spread(target, counts, slot_count):
    return pl.pallas_call(
        spread_kernel,
        grid_spec=pltpu.PrefetchScalarGridSpec(
            num_scalar_prefetch=1,
            grid=(1,),
            in_specs=[pl.BlockSpec(memory_space=pl.ANY)],
            out_specs=pl.BlockSpec(memory_space=pl.ANY),
            scratch_shapes=[
                pltpu.VMEM(counts.shape, counts.dtype),
                pltpu.SemaphoreType.DMA((2, counts.shape[0])),
            ],
        ),
        out_shape=jax.ShapeDtypeStruct((slot_count,) + counts.shape[1:], counts.dtype),
        name="spread",
    )(target, counts)


def parts_of(half, tile):
    end = half + tile
    return [
        [(0, half, half, tile, tile)],
        [(0, 0, half, half, tile)],
        [(0, end, half, half, tile)],
        [(0, half, 0, tile, half)],
        [(0, half, end, tile, half)],
        [(0, 0, 0, half, half), (half, end, 0, half, half)],
        [(0, 0, end, half, half), (half, end, end, half, half)],
    ]


def copies_of(arrays, parts, whole, sems):
    copies = []
    for array, spots in zip(arrays, parts):
        for first, r, c, h, w in spots:
            source = array.at[:, pl.ds(first, h), :]
            copies.append(
                pltpu.make_async_copy(source, whole.at[:, pl.ds(r, h), pl.ds(c, w)], sems.at[len(copies)])
            )
    return copies


def dot(x, y):
    return jnp.dot(x, y, preferred_element_type=jnp.float32)


def place_of(top, left):
    floor = pl.multiple_of(top // 8 * 8, 8)
    base = pl.multiple_of(left // 128 * 128, 128)
    return floor, base, top - floor, left - base


def waves_kernel(count, tops, lefts, probe_all, even_all, odd_all, *refs, points, modes, parts):
    pieces, (half_all, win_all, probe, even, odd, ext, stack, half_buffer, win_buffer, sems, out_sems) = (
        refs[: len(parts)], refs[len(parts) :]
    )
    n = points
    mid = n // 2
    tiles = n // 128
    copies = copies_of(pieces, parts, ext, sems)
    copies += [
        pltpu.make_async_copy(source, held, sems.at[len(copies) + k])
        for k, (source, held) in enumerate(((probe_all, probe), (even_all, even), (odd_all, odd)))
    ]
    for copy in copies:
        copy.start()
    for copy in copies:
        copy.wait()

    def leaving(i):
        slot = lax.rem(i, 2)
        return [
            pltpu.make_async_copy(half_buffer.at[slot], half_all.at[i], out_sems.at[slot, 0]),
            pltpu.make_async_copy(win_buffer.at[slot], win_all.at[i], out_sems.at[slot, 1]),
        ]

    def finish(i):
        @pl.when(i >= 0)
        def _():
            for copy in leaving(jnp.maximum(i, 0)):
                copy.wait()

    @pl.loop(0, count[0])
    def _(i):
        finish(i - 2)
        half_done = half_buffer.at[lax.rem(i, 2)]
        win = win_buffer.at[lax.rem(i, 2)]
        floor, base, low, shift = place_of(tops[i], lefts[i])
        back = lax.rem(128 - shift, 128)
        up = lax.rem(8 - low, 8)
        keep = lax.broadcasted_iota(jnp.int32, (8, 128), 1) < 128 - shift
        upper = lax.broadcasted_iota(jnp.int32, (8, 128), 0) < 8 - low

        def strip(part, g):
            cols = [
                pltpu.roll(ext[part, pl.ds(floor + 8 * g, 8), pl.ds(base + 128 * j, 128)], back, 1)
                for j in range(tiles + 1)
            ]
            vals = [jnp.where(keep, cols[j], cols[j + 1]) for j in range(tiles)]
            return [pltpu.roll(v, up, 0) for v in vals]

        for part in range(2):
            prev = strip(part, 0)
            for g in range(n // 8):
                following = strip(part, g + 1)
                for j in range(tiles):
                    win[part, j, 8 * g : 8 * g + 8, :] = jnp.where(
                        upper, prev[j], following[j]
                    )
                prev = following
        for parity in range(2):
            for r in range(0, mid, 16):
                o_re, o_im = [
                    jnp.concatenate(
                        [win[part, j, pl.ds(2 * r + parity, 16, stride=2), :] for j in range(tiles)], 1
                    )
                    for part in range(2)
                ]
                for m in range(modes):
                    p_re = probe[m, 0, parity, r : r + 16, :]
                    p_im = probe[m, 1, parity, r : r + 16, :]
                    psi_re = (p_re * o_re - p_im * o_im).astype(jnp.bfloat16)
                    psi_im = (p_re * o_im + p_im * o_re).astype(jnp.bfloat16)
                    stack[parity, r : r + 16, m * n : (m + 1) * n] = psi_re
                    stack[parity, mid + r : mid + r + 16, m * n : (m + 1) * n] = psi_im
        for m in range(modes):
            e = dot(even[...], stack[0, :, m * n : (m + 1) * n])
            o = dot(odd[...], stack[1, :, m * n : (m + 1) * n])
            for k, both in enumerate(((e + o).astype(jnp.bfloat16), (e - o).astype(jnp.bfloat16))):
                r = m * n + k * mid
                half_done[r : r + mid, 0:n] = both[:mid]
                half_done[r : r + mid, n : 2 * n] = both[mid:]
        for copy in leaving(i):
            copy.start()

    finish(count[0] - 2)
    finish(count[0] - 1)


def frames_kernel(
    order, count, tops, lefts, raw_all, half_all, win_all,
    probe_all, turn_all, row_even_all, row_odd_all, col_even_all, col_odd_all, res_all, res_t_all,
    pgrad, grad, probe, turn, row_even, row_odd, col_even, col_odd, res, res_t,
    raw_buffer, half_buffer, win_buffer, field, rows, stack, update, amp, sems, const_sems, *, points, modes,
):
    n = points
    mid, quarter = n // 2, n // 4
    tiles = n // 128

    def arriving(i):
        slot = lax.rem(i, 2)
        return [
            pltpu.make_async_copy(half_all.at[i], half_buffer.at[slot], sems.at[slot, 0]),
            pltpu.make_async_copy(raw_all.at[order[i]], raw_buffer.at[slot], sems.at[slot, 1]),
            pltpu.make_async_copy(win_all.at[i], win_buffer.at[slot], sems.at[slot, 2]),
        ]

    def fetch(i):
        @pl.when(i < count[0])
        def _():
            for copy in arriving(i):
                copy.start()

    fetch(0)
    sources = (probe_all, turn_all, row_even_all, row_odd_all, col_even_all, col_odd_all, res_all, res_t_all)
    held = (probe, turn, row_even, row_odd, col_even, col_odd, res, res_t)
    copies = [pltpu.make_async_copy(a, b, const_sems.at[k]) for k, (a, b) in enumerate(zip(sources, held))]
    for copy in copies:
        copy.start()
    grad[...] = jnp.zeros(grad.shape, jnp.float32)
    pgrad[...] = jnp.zeros(pgrad.shape, jnp.float32)
    for copy in copies:
        copy.wait()

    @pl.loop(0, count[0])
    def _(i):
        for copy in arriving(i):
            copy.wait()
        fetch(i + 1)
        slot = lax.rem(i, 2)
        half_done, raw, win = half_buffer.at[slot], raw_buffer.at[slot], win_buffer.at[slot]
        floor, base, low, shift = place_of(tops[i], lefts[i])
        field[...] = dot(half_done[...], turn[...])
        first = dot(res[...], raw[...]).astype(jnp.bfloat16)
        second = dot(first, res_t[...])
        amp[...] = jnp.sqrt(jnp.maximum(second, 0.0)).astype(jnp.bfloat16).astype(jnp.float32)
        for r in range(0, n, 16):
            far = [field[m * n + r : m * n + r + 16, :] for m in range(modes)]
            total = far[0] * far[0]
            for m in range(1, modes):
                total = total + far[m] * far[m]
            scaling = []
            for k in range(2):
                intensity = total[:, 2 * k * mid : (2 * k + 1) * mid] + total[:, (2 * k + 1) * mid : (2 * k + 2) * mid]
                s = 1.0 - amp[r : r + 16, k * mid : (k + 1) * mid] * lax.rsqrt(jnp.maximum(intensity, 1.0))
                scaling += [s, s]
            scaling = jnp.concatenate(scaling, 1)
            for m in range(modes):
                rows[m * n + r : m * n + r + 16, :] = (far[m] * scaling).astype(jnp.bfloat16)
        for m in range(modes):
            e = dot(rows[m * n : (m + 1) * n, 0:n], row_even[...])
            o = dot(rows[m * n : (m + 1) * n, n : 2 * n], row_odd[...])
            for k, both in enumerate(((e + o).astype(jnp.bfloat16), (e - o).astype(jnp.bfloat16))):
                c = m * n + k * mid
                for part in range(2):
                    for block in range(4):
                        r = part * mid + block // 2 * quarter
                        stack[block % 2, r : r + quarter, c : c + mid] = both[
                            block * quarter : (block + 1) * quarter, part * mid : (part + 1) * mid
                        ]
        for m in range(modes):
            c = m * n
            e = dot(col_even[...], stack[0, :, c : c + n])
            o = dot(col_odd[...], stack[1, :, c : c + n])
            for k, both in enumerate((e + o, e - o)):
                update[k * mid : (k + 1) * mid, c : c + n] = both[:mid]
                update[n + k * mid : n + (k + 1) * mid, c : c + n] = both[mid:]
        fresh = lax.broadcasted_iota(jnp.int32, (8, 128), 1) >= shift
        lower = lax.broadcasted_iota(jnp.int32, (8, 128), 0) >= low
        zero = jnp.zeros((8, 128), jnp.float32)
        last = [[zero] * tiles, [zero] * tiles]
        for g in range(n // 8 + 1):
            r = 8 * g
            if g < n // 8:
                o_re, o_im = [
                    jnp.concatenate([win[part, j, r : r + 8, :] for j in range(tiles)], 1) for part in range(2)
                ]
                t_re = t_im = None
                for m in range(modes):
                    u_re = update[r : r + 8, m * n : (m + 1) * n]
                    u_im = update[n + r : n + r + 8, m * n : (m + 1) * n]
                    p_re = probe[m, 0, r : r + 8, :]
                    p_im = probe[m, 1, r : r + 8, :]
                    a_re = p_re * u_re + p_im * u_im
                    a_im = p_re * u_im - p_im * u_re
                    t_re = a_re if t_re is None else t_re + a_re
                    t_im = a_im if t_im is None else t_im + a_im
                    pgrad[m, 0, r : r + 8, :] += o_re * u_re + o_im * u_im
                    pgrad[m, 1, r : r + 8, :] += o_re * u_im - o_im * u_re
                terms = [
                    [pltpu.roll(t[:, 128 * j : 128 * (j + 1)], low, 0) for j in range(tiles)]
                    for t in (t_re, t_im)
                ]
            else:
                terms = [[zero] * tiles, [zero] * tiles]
            for part in range(2):
                placed = [jnp.where(lower, terms[part][j], last[part][j]) for j in range(tiles)]
                turned = [zero] + [pltpu.roll(v, shift, 1) for v in placed] + [zero]
                for j in range(tiles + 1):
                    block = jnp.where(fresh, turned[j + 1], turned[j])
                    grad[part, pl.ds(floor + r, 8), pl.ds(base + 128 * j, 128)] += block
            last = terms

    height, width = grad.shape[1] - NOTE_ROWS, grad.shape[2]
    strips = [(part, r, c) for part in range(2) for c in (0, width - 128) for r in range(0, height, 8)]
    peak = jnp.zeros((8, 128), jnp.float32)
    for part, r, c in strips:
        peak = jnp.maximum(peak, jnp.abs(grad[part, r : r + 8, c : c + 128]))
    power = jnp.ceil(jnp.log2(jnp.full((8, 128), jnp.maximum(jnp.max(peak), 1e-30))))
    factor = jnp.exp2(HEADROOM - power)
    for part, r, c in strips:
        grad[part, r : r + 8, c : c + 128] *= factor
    for part in range(2):
        for c in (0, width - 128):
            for r in range(height, height + NOTE_ROWS, 8):
                grad[part, r : r + 8, c : c + 128] = power


ANYWHERE = pl.BlockSpec(memory_space=pl.ANY)
SCALARS = pl.BlockSpec(memory_space=pltpu.SMEM)
LOCAL = pl.BlockSpec(memory_space=pltpu.VMEM)


def call(kernel, name, ins, outs, in_specs, out_specs, scratch, vmem):
    return pl.pallas_call(
        kernel,
        in_specs=in_specs,
        out_specs=out_specs,
        scratch_shapes=scratch,
        out_shape=outs,
        compiler_params=pltpu.CompilerParams(vmem_limit_bytes=vmem),
        name=name,
    )(*ins)


def exit_waves(slots, count, tops, lefts, probe, pieces, half, tile):
    modes, _, n, _ = probe.shape
    parts = parts_of(half, tile)
    wide = tile + 2 * half
    line = jnp.arange(n, dtype=jnp.int32)
    below = jnp.concatenate([line[0 : n // 2 : 2], line[1 : n // 2 : 2]])
    even = dft_table(below, line[0::2], n, 1)
    odd = dft_table(below, line[1::2], n, 1)
    probe = probe.reshape(modes, 2, n // 2, 2, n).swapaxes(2, 3)
    outs = (
        pltpu.HBM((slots, modes * n, 2 * n), jnp.bfloat16),
        pltpu.HBM((slots, 2, n // 128, n, 128), jnp.float32),
    )
    return call(
        functools.partial(waves_kernel, points=n, modes=modes, parts=parts),
        "waves",
        (count, tops, lefts, probe, even, odd, *pieces),
        outs,
        [SCALARS] * 3 + [ANYWHERE] * (3 + len(parts)),
        [pl.BlockSpec(memory_space=pltpu.HBM)] * 2,
        [pltpu.VMEM(a.shape, a.dtype) for a in (probe, even, odd)]
        + [
            pltpu.VMEM((2, wide, wide), jnp.float32),
            pltpu.VMEM((2, n, modes * n), jnp.bfloat16),
            pltpu.VMEM((2,) + outs[0].shape[1:], outs[0].dtype),
            pltpu.VMEM((2,) + outs[1].shape[1:], outs[1].dtype),
            pltpu.SemaphoreType.DMA((sum(map(len, parts)) + 3,)),
            pltpu.SemaphoreType.DMA((2, 2)),
        ],
        VMEM_BYTES,
    )


def gradients(order, count, tops, lefts, raw, half_done, win, probe, resample, half, tile):
    modes, _, n, _ = probe.shape
    wide = tile + 2 * half
    line = jnp.arange(n, dtype=jnp.int32)
    low = line[: n // 2]
    sides = [line[0::2], line[1::2]]
    turn = jnp.concatenate([dft_table(line, q, n, -1) for q in sides], 1)
    row_even, row_odd = [dft_table(q, low, n, 1) for q in sides]
    col_even, col_odd = [dft_table(low, q, n, -1) for q in sides]
    res = resample.reshape(2, n // 4, 2, n).swapaxes(1, 2).reshape(n, n)
    res_t = resample.reshape(n // 2, 2, n).swapaxes(0, 1).reshape(n, n).T
    outs = [pltpu.VMEM(probe.shape, jnp.float32), pltpu.VMEM((2, wide + NOTE_ROWS, wide), jnp.float32)]
    constant = (probe, turn, row_even, row_odd, col_even, col_odd, res, res_t)
    return call(
        functools.partial(frames_kernel, points=n, modes=modes),
        "frames",
        (order, count, tops, lefts, raw, half_done, win, *constant),
        outs,
        [SCALARS] * 4 + [ANYWHERE] * (3 + len(constant)),
        [LOCAL] * 2,
        [pltpu.VMEM(a.shape, a.dtype) for a in constant]
        + [
            pltpu.VMEM((2, n, n), raw.dtype),
            pltpu.VMEM((2,) + half_done.shape[1:], half_done.dtype),
            pltpu.VMEM((2,) + win.shape[1:], win.dtype),
            pltpu.VMEM((modes * n, 2 * n), jnp.float32),
            pltpu.VMEM((modes * n, 2 * n), jnp.bfloat16),
            pltpu.VMEM((2, n, modes * n), jnp.bfloat16),
            pltpu.VMEM((2 * n, modes * n), jnp.float32),
            pltpu.VMEM((n, n), jnp.float32),
            pltpu.SemaphoreType.DMA((2, 3)),
            pltpu.SemaphoreType.DMA((len(constant),)),
        ],
        VMEM_BYTES,
    )


def to_neighbour(value, axes, step):
    size = lax.axis_size(axes)
    pairs = [(i, i + step) for i in range(size) if 0 <= i + step < size]
    return lax.ppermute(value, axes, pairs)


def merge_kernel(grad, above, below, left, right, out, sem, *, half, tile):
    end = half + tile
    copy = pltpu.make_async_copy(grad.at[:, pl.ds(half, tile), pl.ds(half, tile)], out, sem)
    copy.start()
    copy.wait()
    for part in range(2):
        out[part, :half, :] += above[part]
        out[part, tile - half :, :] += below[part]
        out[part, :, :half] += left[part, half:end, :]
        out[part, :, tile - half :] += right[part, half:end, :]


def merge(grad, pieces, half, tile):
    return call(
        functools.partial(merge_kernel, half=half, tile=tile),
        "merge",
        (grad, *pieces),
        jax.ShapeDtypeStruct((2, tile, tile), jnp.float32),
        [ANYWHERE] + [LOCAL] * 4,
        LOCAL,
        [pltpu.SemaphoreType.DMA],
        16 * 2**20,
    )


def peers(values, axes):
    size = lax.axis_size(axes)
    return [lax.ppermute(v, axes, [(i, i ^ (k + 1)) for i in range(size)]) for k, v in enumerate(values)]


def scattered(value, axes):
    size, place = lax.axis_size(axes), lax.axis_index(axes)
    length = value.shape[0] // size
    parts = [lax.dynamic_slice_in_dim(value, (place ^ k) * length, length, 0) for k in range(size)]
    return sum(peers(parts[1:], axes), parts[0])


def gathered(value, axes):
    size, place = lax.axis_size(axes), lax.axis_index(axes)
    held = [value] + peers([value] * (size - 1), axes)
    parts = []
    for j in range(size):
        part = held[size - 1]
        for k in range(size - 1):
            part = jnp.where(place == j ^ k, held[k], part)
        parts.append(part)
    return jnp.concatenate(parts, 0)


def summed(value, axes):
    held = [value] + peers([value] * (lax.axis_size(axes) - 1), axes)
    while len(held) > 1:
        held = [a + b for a, b in zip(held[::2], held[1::2])]
    return held[0]


def shards(object_field, probe, raw_counts, resample_delta, tile_row, offsets):
    modes, _, points, _ = probe.shape
    half = points // 2
    tile = object_field.shape[1]
    tile_rows = lax.axis_size(ROW)
    frame_total = raw_counts.shape[0] * tile_rows * lax.axis_size(COL)
    above = to_neighbour(object_field[:, tile - half :, :], ROW, 1)
    below = to_neighbour(object_field[:, :half, :], ROW, -1)
    left = to_neighbour(object_field[:, :, tile - half :], COL, 1)
    right = to_neighbour(object_field[:, :, :half], COL, -1)
    corners = [
        jnp.concatenate([a[:, :, cols] for a in (above, below)], 1)
        for cols in (slice(tile - half, None), slice(0, half))
    ]
    corners = [to_neighbour(a, COL, step) for a, step in zip(corners, (1, -1))]
    target = tile_row[:, 0]
    raw_counts, corners = lax.optimization_barrier((raw_counts, corners))
    slots = spread(target, raw_counts, tile_rows)
    arrived = lax.all_to_all(slots, ROW, split_axis=0, concat_axis=0, tiled=True)
    slot_ids = jnp.arange(tile_rows, dtype=jnp.int32)
    picks = (target[:, None] == slot_ids[None, :]).astype(jnp.int32)
    requests = jnp.stack(
        [jnp.sum(picks * offsets[:, 0:1], 0), jnp.sum(picks * offsets[:, 1:2], 0), jnp.sum(picks, 0)], 1
    )
    received = lax.all_to_all(requests, ROW, split_axis=0, concat_axis=0, tiled=True)
    live = received[:, 2]
    count = jnp.sum(live)
    rank = jnp.sum(jnp.where(slot_ids[None, :] < slot_ids[:, None], live[None, :], 0), 1)
    place = jnp.minimum(slot_ids, jnp.maximum(count - 1, 0))
    hit = (rank[None, :] == place[:, None]) & (live[None, :] > 0)
    order = jnp.sum(jnp.where(hit, slot_ids[None, :], 0), 1)
    tops = jnp.sum(jnp.where(hit, received[None, :, 0], 0), 1)
    lefts = jnp.sum(jnp.where(hit, received[None, :, 1], 0), 1)
    count = count[None]
    resample = (jnp.eye(points, dtype=jnp.float32) + resample_delta).astype(jnp.bfloat16)
    pieces = [object_field, above, below, left, right, *corners]
    half_done, win = exit_waves(tile_rows, count, tops, lefts, probe, pieces, half, tile)
    probe_total, grad = gradients(
        order, count, tops, lefts, arrived, half_done, win, probe, resample, half, tile
    )
    total = scattered(probe_total.reshape(-1, points), "core")
    from_west = to_neighbour(grad[:, :, half + tile :].astype(jnp.float16), COL, 1)
    from_east = to_neighbour(grad[:, :, :half].astype(jnp.float16), COL, -1)
    total = scattered(scattered(total, "x"), "z")
    total = summed(total, ("y_far", "y_near")) * (1.0 / math.sqrt(frame_total))
    total, from_west, from_east = lax.optimization_barrier((total, from_west, from_east))
    from_west, from_east = [
        strip[:, :-NOTE_ROWS, :].astype(jnp.float32) * jnp.exp2(strip[0, -1, 0].astype(jnp.float32) - HEADROOM)
        for strip in (from_west, from_east)
    ]

    def with_corners(rows):
        strip = grad[:, rows, half : half + tile]
        strip = strip.at[:, :, :half].add(from_west[:, rows, :])
        return strip.at[:, :, tile - half :].add(from_east[:, rows, :])

    from_below = to_neighbour(with_corners(slice(0, half)), ROW, -1)
    from_above = to_neighbour(with_corners(slice(half + tile, 2 * half + tile)), ROW, 1)
    total = gathered(gathered(total, "z"), "x")
    total, from_above, from_below = lax.optimization_barrier((total, from_above, from_below))
    total = gathered(total, "core")
    object_grad = merge(grad, [from_above, from_below, from_west, from_east], half, tile)
    return (object_grad, total.reshape(probe.shape))


def solution(mesh):
    torus = Mesh(mesh.devices.reshape(4, 2, 2, 4, 2), ROW_COL)
    return jax.shard_map(
        shards,
        mesh=torus,
        in_specs=(
            P(None, ROW, COL),
            P(),
            P(ROW_COL, None, None),
            P(),
            P(ROW_COL, None),
            P(ROW_COL, None),
        ),
        out_specs=(P(None, ROW, COL), P()),
        check_vma=False,
    )
```

```python
import functools
import math

import jax
import jax.numpy as jnp
from jax import lax
from jax.experimental import pallas as pl
from jax.experimental.pallas import tpu as pltpu
from jax.sharding import Mesh
from jax.sharding import PartitionSpec as P

ROW = ("x", "y_far", "core")
COL = ("z", "y_near")
ROW_COL = ROW + COL
VMEM_BYTES = 52 * 2**20
HEADROOM = 14.0
NOTE_ROWS = 16


def dft_table(left, right, points, sign):
    phases = left[:, None] * right[None, :] % points
    angles = phases.astype(jnp.float32) * (2.0 * math.pi / points)
    norming = 1.0 / math.sqrt(points)
    cosine = jnp.cos(angles) * norming
    sine_part = -jnp.sin(angles) * norming * sign
    table = jnp.concatenate(
        [jnp.concatenate([cosine, -sine_part], 1), jnp.concatenate([sine_part, cosine], 1)], 0
    )
    return table.astype(jnp.bfloat16)


def spread_kernel(target, counts, slots, held, sems):
    count = counts.shape[0]
    inward = [pltpu.make_async_copy(counts.at[j], held.at[j], sems.at[0, j]) for j in range(count)]
    outward = [pltpu.make_async_copy(held.at[j], slots.at[target[j]], sems.at[1, j]) for j in range(count)]
    for copy in inward:
        copy.start()
    for j in range(count):
        inward[j].wait()
        outward[j].start()
    for copy in outward:
        copy.wait()


def spread(target, counts, slot_count):
    return pl.pallas_call(
        spread_kernel,
        grid_spec=pltpu.PrefetchScalarGridSpec(
            num_scalar_prefetch=1,
            grid=(1,),
            in_specs=[pl.BlockSpec(memory_space=pl.ANY)],
            out_specs=pl.BlockSpec(memory_space=pl.ANY),
            scratch_shapes=[
                pltpu.VMEM(counts.shape, counts.dtype),
                pltpu.SemaphoreType.DMA((2, counts.shape[0])),
            ],
        ),
        out_shape=jax.ShapeDtypeStruct((slot_count,) + counts.shape[1:], counts.dtype),
        name="spread",
    )(target, counts)


def parts_of(half, tile):
    end = half + tile
    return [
        [(0, half, half, tile, tile)],
        [(0, 0, half, half, tile)],
        [(0, end, half, half, tile)],
        [(0, half, 0, tile, half)],
        [(0, half, end, tile, half)],
        [(0, 0, 0, half, half), (half, end, 0, half, half)],
        [(0, 0, end, half, half), (half, end, end, half, half)],
    ]


def copies_of(arrays, parts, whole, sems):
    copies = []
    for array, spots in zip(arrays, parts):
        for first, r, c, h, w in spots:
            source = array.at[:, pl.ds(first, h), :]
            copies.append(
                pltpu.make_async_copy(source, whole.at[:, pl.ds(r, h), pl.ds(c, w)], sems.at[len(copies)])
            )
    return copies


def dot(x, y):
    return jnp.dot(x, y, preferred_element_type=jnp.float32)


def place_of(top, left):
    floor = pl.multiple_of(top // 8 * 8, 8)
    base = pl.multiple_of(left // 128 * 128, 128)
    return floor, base, top - floor, left - base


def waves_kernel(count, tops, lefts, probe_all, even_all, odd_all, *refs, points, modes, parts):
    pieces, (half_all, win_all, probe, even, odd, ext, stack, half_buffer, win_buffer, sems, out_sems) = (
        refs[: len(parts)], refs[len(parts) :]
    )
    n = points
    mid = n // 2
    tiles = n // 128
    copies = copies_of(pieces, parts, ext, sems)
    copies += [
        pltpu.make_async_copy(source, held, sems.at[len(copies) + k])
        for k, (source, held) in enumerate(((probe_all, probe), (even_all, even), (odd_all, odd)))
    ]
    for copy in copies:
        copy.start()
    for copy in copies:
        copy.wait()

    def leaving(i):
        slot = lax.rem(i, 2)
        return [
            pltpu.make_async_copy(half_buffer.at[slot], half_all.at[i], out_sems.at[slot, 0]),
            pltpu.make_async_copy(win_buffer.at[slot], win_all.at[i], out_sems.at[slot, 1]),
        ]

    def finish(i):
        @pl.when(i >= 0)
        def _():
            for copy in leaving(jnp.maximum(i, 0)):
                copy.wait()

    @pl.loop(0, count[0])
    def _(i):
        finish(i - 2)
        half_done = half_buffer.at[lax.rem(i, 2)]
        win = win_buffer.at[lax.rem(i, 2)]
        floor, base, low, shift = place_of(tops[i], lefts[i])
        back = lax.rem(128 - shift, 128)
        up = lax.rem(8 - low, 8)
        keep = lax.broadcasted_iota(jnp.int32, (8, 128), 1) < 128 - shift
        upper = lax.broadcasted_iota(jnp.int32, (8, 128), 0) < 8 - low

        def strip(part, g):
            cols = [
                pltpu.roll(ext[part, pl.ds(floor + 8 * g, 8), pl.ds(base + 128 * j, 128)], back, 1)
                for j in range(tiles + 1)
            ]
            vals = [jnp.where(keep, cols[j], cols[j + 1]) for j in range(tiles)]
            return [pltpu.roll(v, up, 0) for v in vals]

        for part in range(2):
            prev = strip(part, 0)
            for g in range(n // 8):
                following = strip(part, g + 1)
                for j in range(tiles):
                    win[part, j, 8 * g : 8 * g + 8, :] = jnp.where(
                        upper, prev[j], following[j]
                    )
                prev = following
        for parity in range(2):
            for r in range(0, mid, 16):
                o_re, o_im = [
                    jnp.concatenate(
                        [win[part, j, pl.ds(2 * r + parity, 16, stride=2), :] for j in range(tiles)], 1
                    )
                    for part in range(2)
                ]
                for m in range(modes):
                    p_re = probe[m, 0, parity, r : r + 16, :]
                    p_im = probe[m, 1, parity, r : r + 16, :]
                    psi_re = (p_re * o_re - p_im * o_im).astype(jnp.bfloat16)
                    psi_im = (p_re * o_im + p_im * o_re).astype(jnp.bfloat16)
                    stack[parity, r : r + 16, m * n : (m + 1) * n] = psi_re
                    stack[parity, mid + r : mid + r + 16, m * n : (m + 1) * n] = psi_im
        for m in range(modes):
            e = dot(even[...], stack[0, :, m * n : (m + 1) * n])
            o = dot(odd[...], stack[1, :, m * n : (m + 1) * n])
            for k, both in enumerate(((e + o).astype(jnp.bfloat16), (e - o).astype(jnp.bfloat16))):
                r = m * n + k * mid
                half_done[r : r + mid, 0:n] = both[:mid]
                half_done[r : r + mid, n : 2 * n] = both[mid:]
        for copy in leaving(i):
            copy.start()

    finish(count[0] - 2)
    finish(count[0] - 1)


def frames_kernel(
    order, count, tops, lefts, raw_all, half_all, win_all,
    probe_all, turn_all, row_even_all, row_odd_all, col_even_all, col_odd_all, res_all, res_t_all,
    pgrad, grad, probe, turn, row_even, row_odd, col_even, col_odd, res, res_t,
    raw_buffer, half_buffer, win_buffer, field, rows, stack, update, amp, sems, const_sems, *, points, modes,
):
    n = points
    mid, quarter = n // 2, n // 4
    tiles = n // 128

    def arriving(i):
        slot = lax.rem(i, 3)
        return [
            pltpu.make_async_copy(half_all.at[i], half_buffer.at[slot], sems.at[slot, 0]),
            pltpu.make_async_copy(raw_all.at[order[i]], raw_buffer.at[slot], sems.at[slot, 1]),
            pltpu.make_async_copy(win_all.at[i], win_buffer.at[slot], sems.at[slot, 2]),
        ]

    def fetch(i):
        @pl.when(i < count[0])
        def _():
            for copy in arriving(i):
                copy.start()

    fetch(0)
    sources = (probe_all, turn_all, row_even_all, row_odd_all, col_even_all, col_odd_all, res_all, res_t_all)
    held = (probe, turn, row_even, row_odd, col_even, col_odd, res, res_t)
    copies = [pltpu.make_async_copy(a, b, const_sems.at[k]) for k, (a, b) in enumerate(zip(sources, held))]
    for copy in copies:
        copy.start()
    grad[...] = jnp.zeros(grad.shape, jnp.float32)
    pgrad[...] = jnp.zeros(pgrad.shape, jnp.float32)
    for copy in copies:
        copy.wait()

    update[...] = jnp.zeros(update.shape, jnp.float32)
    win_buffer[2] = jnp.zeros(win_buffer.shape[1:], jnp.float32)

    def collect(i):
        win = win_buffer.at[lax.rem(i + 3, 3)]
        at = jnp.maximum(i, 0)
        floor, base, low, shift = place_of(tops[at], lefts[at])
        fresh = lax.broadcasted_iota(jnp.int32, (8, 128), 1) >= shift
        lower = lax.broadcasted_iota(jnp.int32, (8, 128), 0) >= low
        zero = jnp.zeros((8, 128), jnp.float32)
        last = [[zero] * tiles, [zero] * tiles]
        for g in range(n // 8 + 1):
            r = 8 * g
            if g < n // 8:
                o_re, o_im = [
                    jnp.concatenate([win[part, j, r : r + 8, :] for j in range(tiles)], 1) for part in range(2)
                ]
                t_re = t_im = None
                for m in range(modes):
                    u_re = update[r : r + 8, m * n : (m + 1) * n]
                    u_im = update[n + r : n + r + 8, m * n : (m + 1) * n]
                    p_re = probe[m, 0, r : r + 8, :]
                    p_im = probe[m, 1, r : r + 8, :]
                    a_re = p_re * u_re + p_im * u_im
                    a_im = p_re * u_im - p_im * u_re
                    t_re = a_re if t_re is None else t_re + a_re
                    t_im = a_im if t_im is None else t_im + a_im
                    pgrad[m, 0, r : r + 8, :] += o_re * u_re + o_im * u_im
                    pgrad[m, 1, r : r + 8, :] += o_re * u_im - o_im * u_re
                terms = [
                    [pltpu.roll(t[:, 128 * j : 128 * (j + 1)], low, 0) for j in range(tiles)]
                    for t in (t_re, t_im)
                ]
            else:
                terms = [[zero] * tiles, [zero] * tiles]
            for part in range(2):
                placed = [jnp.where(lower, terms[part][j], last[part][j]) for j in range(tiles)]
                turned = [zero] + [pltpu.roll(v, shift, 1) for v in placed] + [zero]
                for j in range(tiles + 1):
                    block = jnp.where(fresh, turned[j + 1], turned[j])
                    grad[part, pl.ds(floor + r, 8), pl.ds(base + 128 * j, 128)] += block
            last = terms

    @pl.loop(0, count[0])
    def _(i):
        for copy in arriving(i):
            copy.wait()
        fetch(i + 1)
        slot = lax.rem(i, 3)
        half_done, raw = half_buffer.at[slot], raw_buffer.at[slot]
        field[...] = dot(half_done[...], turn[...])
        collect(i - 1)
        first = dot(res[...], raw[...]).astype(jnp.bfloat16)
        second = dot(first, res_t[...])
        amp[...] = jnp.sqrt(jnp.maximum(second, 0.0)).astype(jnp.bfloat16).astype(jnp.float32)
        for r in range(0, n, 16):
            far = [field[m * n + r : m * n + r + 16, :] for m in range(modes)]
            total = far[0] * far[0]
            for m in range(1, modes):
                total = total + far[m] * far[m]
            scaling = []
            for k in range(2):
                intensity = total[:, 2 * k * mid : (2 * k + 1) * mid] + total[:, (2 * k + 1) * mid : (2 * k + 2) * mid]
                s = 1.0 - amp[r : r + 16, k * mid : (k + 1) * mid] * lax.rsqrt(jnp.maximum(intensity, 1.0))
                scaling += [s, s]
            scaling = jnp.concatenate(scaling, 1)
            for m in range(modes):
                rows[m * n + r : m * n + r + 16, :] = (far[m] * scaling).astype(jnp.bfloat16)
        for m in range(modes):
            e = dot(rows[m * n : (m + 1) * n, 0:n], row_even[...])
            o = dot(rows[m * n : (m + 1) * n, n : 2 * n], row_odd[...])
            for k, both in enumerate(((e + o).astype(jnp.bfloat16), (e - o).astype(jnp.bfloat16))):
                c = m * n + k * mid
                for part in range(2):
                    for block in range(4):
                        r = part * mid + block // 2 * quarter
                        stack[block % 2, r : r + quarter, c : c + mid] = both[
                            block * quarter : (block + 1) * quarter, part * mid : (part + 1) * mid
                        ]
        for m in range(modes):
            c = m * n
            e = dot(col_even[...], stack[0, :, c : c + n])
            o = dot(col_odd[...], stack[1, :, c : c + n])
            for k, both in enumerate((e + o, e - o)):
                update[k * mid : (k + 1) * mid, c : c + n] = both[:mid]
                update[n + k * mid : n + (k + 1) * mid, c : c + n] = both[mid:]

    @pl.when(count[0] > 0)
    def _():
        collect(count[0] - 1)

    height, width = grad.shape[1] - NOTE_ROWS, grad.shape[2]
    strips = [(part, r, c) for part in range(2) for c in (0, width - 128) for r in range(0, height, 8)]
    peak = jnp.zeros((8, 128), jnp.float32)
    for part, r, c in strips:
        peak = jnp.maximum(peak, jnp.abs(grad[part, r : r + 8, c : c + 128]))
    power = jnp.ceil(jnp.log2(jnp.full((8, 128), jnp.maximum(jnp.max(peak), 1e-30))))
    factor = jnp.exp2(HEADROOM - power)
    for part, r, c in strips:
        grad[part, r : r + 8, c : c + 128] *= factor
    for part in range(2):
        for c in (0, width - 128):
            for r in range(height, height + NOTE_ROWS, 8):
                grad[part, r : r + 8, c : c + 128] = power


ANYWHERE = pl.BlockSpec(memory_space=pl.ANY)
SCALARS = pl.BlockSpec(memory_space=pltpu.SMEM)
LOCAL = pl.BlockSpec(memory_space=pltpu.VMEM)


def call(kernel, name, ins, outs, in_specs, out_specs, scratch, vmem):
    return pl.pallas_call(
        kernel,
        in_specs=in_specs,
        out_specs=out_specs,
        scratch_shapes=scratch,
        out_shape=outs,
        compiler_params=pltpu.CompilerParams(vmem_limit_bytes=vmem),
        name=name,
    )(*ins)


def exit_waves(slots, count, tops, lefts, probe, pieces, half, tile):
    modes, _, n, _ = probe.shape
    parts = parts_of(half, tile)
    wide = tile + 2 * half
    line = jnp.arange(n, dtype=jnp.int32)
    below = jnp.concatenate([line[0 : n // 2 : 2], line[1 : n // 2 : 2]])
    even = dft_table(below, line[0::2], n, 1)
    odd = dft_table(below, line[1::2], n, 1)
    probe = probe.reshape(modes, 2, n // 2, 2, n).swapaxes(2, 3)
    outs = (
        pltpu.HBM((slots, modes * n, 2 * n), jnp.bfloat16),
        pltpu.HBM((slots, 2, n // 128, n, 128), jnp.float32),
    )
    return call(
        functools.partial(waves_kernel, points=n, modes=modes, parts=parts),
        "waves",
        (count, tops, lefts, probe, even, odd, *pieces),
        outs,
        [SCALARS] * 3 + [ANYWHERE] * (3 + len(parts)),
        [pl.BlockSpec(memory_space=pltpu.HBM)] * 2,
        [pltpu.VMEM(a.shape, a.dtype) for a in (probe, even, odd)]
        + [
            pltpu.VMEM((2, wide, wide), jnp.float32),
            pltpu.VMEM((2, n, modes * n), jnp.bfloat16),
            pltpu.VMEM((2,) + outs[0].shape[1:], outs[0].dtype),
            pltpu.VMEM((2,) + outs[1].shape[1:], outs[1].dtype),
            pltpu.SemaphoreType.DMA((sum(map(len, parts)) + 3,)),
            pltpu.SemaphoreType.DMA((2, 2)),
        ],
        VMEM_BYTES,
    )


def gradients(order, count, tops, lefts, raw, half_done, win, probe, resample, half, tile):
    modes, _, n, _ = probe.shape
    wide = tile + 2 * half
    line = jnp.arange(n, dtype=jnp.int32)
    low = line[: n // 2]
    sides = [line[0::2], line[1::2]]
    turn = jnp.concatenate([dft_table(line, q, n, -1) for q in sides], 1)
    row_even, row_odd = [dft_table(q, low, n, 1) for q in sides]
    col_even, col_odd = [dft_table(low, q, n, -1) for q in sides]
    res = resample.reshape(2, n // 4, 2, n).swapaxes(1, 2).reshape(n, n)
    res_t = resample.reshape(n // 2, 2, n).swapaxes(0, 1).reshape(n, n).T
    outs = [pltpu.VMEM(probe.shape, jnp.float32), pltpu.VMEM((2, wide + NOTE_ROWS, wide), jnp.float32)]
    constant = (probe, turn, row_even, row_odd, col_even, col_odd, res, res_t)
    return call(
        functools.partial(frames_kernel, points=n, modes=modes),
        "frames",
        (order, count, tops, lefts, raw, half_done, win, *constant),
        outs,
        [SCALARS] * 4 + [ANYWHERE] * (3 + len(constant)),
        [LOCAL] * 2,
        [pltpu.VMEM(a.shape, a.dtype) for a in constant]
        + [
            pltpu.VMEM((3, n, n), raw.dtype),
            pltpu.VMEM((3,) + half_done.shape[1:], half_done.dtype),
            pltpu.VMEM((3,) + win.shape[1:], win.dtype),
            pltpu.VMEM((modes * n, 2 * n), jnp.float32),
            pltpu.VMEM((modes * n, 2 * n), jnp.bfloat16),
            pltpu.VMEM((2, n, modes * n), jnp.bfloat16),
            pltpu.VMEM((2 * n, modes * n), jnp.float32),
            pltpu.VMEM((n, n), jnp.float32),
            pltpu.SemaphoreType.DMA((3, 3)),
            pltpu.SemaphoreType.DMA((len(constant),)),
        ],
        VMEM_BYTES,
    )


def to_neighbour(value, axes, step):
    size = lax.axis_size(axes)
    pairs = [(i, i + step) for i in range(size) if 0 <= i + step < size]
    return lax.ppermute(value, axes, pairs)


def merge_kernel(grad, above, below, left, right, out, sem, *, half, tile):
    end = half + tile
    copy = pltpu.make_async_copy(grad.at[:, pl.ds(half, tile), pl.ds(half, tile)], out, sem)
    copy.start()
    copy.wait()
    for part in range(2):
        out[part, :half, :] += above[part]
        out[part, tile - half :, :] += below[part]
        out[part, :, :half] += left[part, half:end, :]
        out[part, :, tile - half :] += right[part, half:end, :]


def merge(grad, pieces, half, tile):
    return call(
        functools.partial(merge_kernel, half=half, tile=tile),
        "merge",
        (grad, *pieces),
        jax.ShapeDtypeStruct((2, tile, tile), jnp.float32),
        [ANYWHERE] + [LOCAL] * 4,
        LOCAL,
        [pltpu.SemaphoreType.DMA],
        16 * 2**20,
    )


def peers(values, axes):
    size = lax.axis_size(axes)
    return [lax.ppermute(v, axes, [(i, i ^ (k + 1)) for i in range(size)]) for k, v in enumerate(values)]


def scattered(value, axes):
    size, place = lax.axis_size(axes), lax.axis_index(axes)
    length = value.shape[0] // size
    parts = [lax.dynamic_slice_in_dim(value, (place ^ k) * length, length, 0) for k in range(size)]
    return sum(peers(parts[1:], axes), parts[0])


def gathered(value, axes):
    size, place = lax.axis_size(axes), lax.axis_index(axes)
    held = [value] + peers([value] * (size - 1), axes)
    parts = []
    for j in range(size):
        part = held[size - 1]
        for k in range(size - 1):
            part = jnp.where(place == j ^ k, held[k], part)
        parts.append(part)
    return jnp.concatenate(parts, 0)


def summed(value, axes):
    held = [value] + peers([value] * (lax.axis_size(axes) - 1), axes)
    while len(held) > 1:
        held = [a + b for a, b in zip(held[::2], held[1::2])]
    return held[0]


def shards(object_field, probe, raw_counts, resample_delta, tile_row, offsets):
    modes, _, points, _ = probe.shape
    half = points // 2
    tile = object_field.shape[1]
    tile_rows = lax.axis_size(ROW)
    frame_total = raw_counts.shape[0] * tile_rows * lax.axis_size(COL)
    above = to_neighbour(object_field[:, tile - half :, :], ROW, 1)
    below = to_neighbour(object_field[:, :half, :], ROW, -1)
    left = to_neighbour(object_field[:, :, tile - half :], COL, 1)
    right = to_neighbour(object_field[:, :, :half], COL, -1)
    corners = [
        jnp.concatenate([a[:, :, cols] for a in (above, below)], 1)
        for cols in (slice(tile - half, None), slice(0, half))
    ]
    corners = [to_neighbour(a, COL, step) for a, step in zip(corners, (1, -1))]
    target = tile_row[:, 0]
    raw_counts, corners = lax.optimization_barrier((raw_counts, corners))
    slots = spread(target, raw_counts, tile_rows)
    arrived = lax.all_to_all(slots, ROW, split_axis=0, concat_axis=0, tiled=True)
    slot_ids = jnp.arange(tile_rows, dtype=jnp.int32)
    picks = (target[:, None] == slot_ids[None, :]).astype(jnp.int32)
    requests = jnp.stack(
        [jnp.sum(picks * offsets[:, 0:1], 0), jnp.sum(picks * offsets[:, 1:2], 0), jnp.sum(picks, 0)], 1
    )
    received = lax.all_to_all(requests, ROW, split_axis=0, concat_axis=0, tiled=True)
    live = received[:, 2]
    count = jnp.sum(live)
    rank = jnp.sum(jnp.where(slot_ids[None, :] < slot_ids[:, None], live[None, :], 0), 1)
    place = jnp.minimum(slot_ids, jnp.maximum(count - 1, 0))
    hit = (rank[None, :] == place[:, None]) & (live[None, :] > 0)
    order = jnp.sum(jnp.where(hit, slot_ids[None, :], 0), 1)
    tops = jnp.sum(jnp.where(hit, received[None, :, 0], 0), 1)
    lefts = jnp.sum(jnp.where(hit, received[None, :, 1], 0), 1)
    count = count[None]
    resample = (jnp.eye(points, dtype=jnp.float32) + resample_delta).astype(jnp.bfloat16)
    pieces = [object_field, above, below, left, right, *corners]
    half_done, win = exit_waves(tile_rows, count, tops, lefts, probe, pieces, half, tile)
    probe_total, grad = gradients(
        order, count, tops, lefts, arrived, half_done, win, probe, resample, half, tile
    )
    total = scattered(probe_total.reshape(-1, points), "core")
    from_west = to_neighbour(grad[:, :, half + tile :].astype(jnp.float16), COL, 1)
    from_east = to_neighbour(grad[:, :, :half].astype(jnp.float16), COL, -1)
    total = scattered(scattered(total, "x"), "z")
    total = summed(total, ("y_far", "y_near")) * (1.0 / math.sqrt(frame_total))
    total, from_west, from_east = lax.optimization_barrier((total, from_west, from_east))
    from_west, from_east = [
        strip[:, :-NOTE_ROWS, :].astype(jnp.float32) * jnp.exp2(strip[0, -1, 0].astype(jnp.float32) - HEADROOM)
        for strip in (from_west, from_east)
    ]

    def with_corners(rows):
        strip = grad[:, rows, half : half + tile]
        strip = strip.at[:, :, :half].add(from_west[:, rows, :])
        return strip.at[:, :, tile - half :].add(from_east[:, rows, :])

    from_below = to_neighbour(with_corners(slice(0, half)), ROW, -1)
    from_above = to_neighbour(with_corners(slice(half + tile, 2 * half + tile)), ROW, 1)
    total = gathered(gathered(total, "z"), "x")
    total, from_above, from_below = lax.optimization_barrier((total, from_above, from_below))
    total = gathered(total, "core")
    object_grad = merge(grad, [from_above, from_below, from_west, from_east], half, tile)
    return (object_grad, total.reshape(probe.shape))


def solution(mesh):
    torus = Mesh(mesh.devices.reshape(4, 2, 2, 4, 2), ROW_COL)
    return jax.shard_map(
        shards,
        mesh=torus,
        in_specs=(
            P(None, ROW, COL),
            P(),
            P(ROW_COL, None, None),
            P(),
            P(ROW_COL, None),
            P(ROW_COL, None),
        ),
        out_specs=(P(None, ROW, COL), P()),
        check_vma=False,
    )
```
